32 devices in a mesh: row: 8 (over y, x, core), col: 4 (over z).
Axes of the slice: x: 2, y: 2, z: 4, core: 2. Of those that a mesh axis runs over, the one named last changes fastest.
Arguments:
- front_matrix: bfloat16 [20480, 20480], P('row', 'col'), may hold values from -37 to 37
- right_samples: bfloat16 [20480, 256], P('col'), may hold values from -0.0390625 to 0.0390625
- left_samples: bfloat16 [20480, 256], P('row'), may hold values from -0.0390625 to 0.0390625
Outputs:
- residual: bfloat16 [20480, 20480], P('row', 'col')
- core_scaled: float32 [256, 256], replicated
The draws below stay inside these ranges and needn't reach their ends.
All inputs are finite; a program needn't handle non-finite values.
Results may differ from the reference program's by a relative error of at most 0.0035.
Values may be sent and summed in bfloat16 or wider, within the bound.
A program may use at most 128 MiB of HBM per device.

```python
import math
import jax
import jax.numpy as jnp
from jax import lax

ORDER = 20480
SAMPLES = 256
N_ROW = 8


def draw_front_matrix(key, part):
    keys = jax.random.split(jax.random.fold_in(key, 17), 6)
    row_scale = jnp.exp(jax.random.uniform(keys[0], (ORDER,), jnp.float32, math.log(0.05), math.log(0.5)))
    segment = ORDER // 8
    offsets = jax.random.randint(keys[5], (8,), 0, segment)
    heavy_rows = (jnp.arange(8) * segment + offsets).astype(jnp.int32)
    row_scale = row_scale.at[heavy_rows].set(3.0)
    col_scale = jnp.exp(jax.random.uniform(keys[1], (ORDER,), jnp.float32, math.log(0.3), math.log(3.0)))
    base = jnp.clip(jax.random.normal(keys[2], (ORDER, ORDER), jnp.float32), -4.0, 4.0)
    values = base * row_scale[:, None] * col_scale[None, :]
    return values.astype(jnp.bfloat16)


def block_levels(rng, extent, cuts, smallest, high):
    def one(dim, parts):
        draws = jax.random.uniform(jax.random.fold_in(jax.random.fold_in(rng, 6), dim), (parts,), jnp.float32, smallest / len(cuts), high / len(cuts))
        return jnp.repeat(jnp.exp(draws), extent[dim] // parts).reshape((-1,) + (1,) * (len(extent) - dim - 1))

    loudness = one(*cuts[0])
    for cut in cuts[1:]:
        loudness = loudness * one(*cut)
    return loudness


def bell_draw(own_key, dims, spread, most, cuts=(), dtype=jnp.bfloat16):
    gain = block_levels(own_key, dims, cuts, -0.22, 0.18) if cuts else 1.0
    result = jax.random.normal(own_key, dims, jnp.float32) * spread * gain
    return jnp.minimum(jnp.maximum(result, -most), most).astype(dtype)


def setup_inputs(seed: int = 0) -> dict:
    splits = jax.random.split(jax.random.key(seed), 4)
    front_matrix = draw_front_matrix(jax.random.fold_in(splits[3], 71), 0)
    right_samples = bell_draw(splits[1], (ORDER, SAMPLES), ORDER ** -0.5, 0.0390625, ((0, 4),))
    left_samples = bell_draw(splits[2], (ORDER, SAMPLES), ORDER ** -0.5, 0.0390625, ((0, 8),))
    return dict(front_matrix=front_matrix, right_samples=right_samples, left_samples=left_samples)


def orthonormal(sketch):
    gram_matrix = lax.dot_general(sketch.astype(jnp.float32), sketch.astype(jnp.float32), (((0,), (0,)), ((), ())), precision=lax.Precision.HIGHEST, preferred_element_type=jnp.float32)
    lower_factor = jnp.linalg.cholesky(gram_matrix)
    return jax.scipy.linalg.solve_triangular(lower_factor, sketch.T, lower=True).T

def reference(front_matrix, right_samples, left_samples):
    sketch_rows = jnp.dot(front_matrix.astype(jnp.float32), right_samples.astype(jnp.float32), preferred_element_type=jnp.float32)
    sketch_cols = lax.dot_general(front_matrix.astype(jnp.float32), left_samples.astype(jnp.float32), (((0,), (0,)), ((), ())), preferred_element_type=jnp.float32)
    basis_rows = orthonormal(sketch_rows).astype(jnp.bfloat16)
    basis_cols = orthonormal(sketch_cols).astype(jnp.bfloat16)
    applied = jnp.dot(front_matrix.astype(jnp.float32), basis_cols.astype(jnp.float32), preferred_element_type=jnp.float32)
    core_matrix = lax.dot_general(basis_rows.astype(jnp.float32), applied.astype(jnp.float32), (((0,), (0,)), ((), ())), precision=lax.Precision.HIGHEST, preferred_element_type=jnp.float32)
    core_scaled = core_matrix / jnp.sqrt(jnp.float32(ORDER))
    projected = jnp.dot(basis_rows.astype(jnp.float32), core_matrix.astype(jnp.float32), precision=lax.Precision.HIGHEST, preferred_element_type=jnp.float32).astype(jnp.bfloat16)
    row_blocks = front_matrix.reshape(N_ROW, ORDER // N_ROW, ORDER)
    proj_blocks = projected.reshape(N_ROW, ORDER // N_ROW, SAMPLES)

    def update_block(pair):
        block_front, block_proj = pair
        update = lax.dot_general(block_proj.astype(jnp.float32), basis_cols.astype(jnp.float32), (((1,), (1,)), ((), ())), preferred_element_type=jnp.float32)
        return (block_front.astype(jnp.float32) - update).astype(jnp.bfloat16)
    residual = lax.map(update_block, (row_blocks, proj_blocks)).reshape(ORDER, ORDER)
    return (residual, core_scaled)
```

```python
import functools

import jax
import jax.numpy as jnp
from jax import lax
from jax.experimental import pallas as pl
from jax.experimental.pallas import tpu as pltpu
from jax.sharding import PartitionSpec as P

F32 = jnp.float32
BF16 = jnp.bfloat16
BASE = 64


def mm(a, b, dims=((1,), (0,))):
    return lax.dot_general(
        a, b, (dims, ((), ())), precision=lax.Precision.HIGHEST, preferred_element_type=F32
    )


def base_inverse(grams):
    size = grams[0].shape[0]
    tall = size // 8
    width = 2 * size
    eye = (
        lax.broadcasted_iota(jnp.int32, (size, size), 0) == lax.broadcasted_iota(jnp.int32, (size, size), 1)
    ).astype(F32)
    wide = [jnp.concatenate([g, eye], axis=1) for g in grams]
    parts = [[w[8 * t : 8 * t + 8] for t in range(tall)] for w in wide]
    sub = lax.broadcasted_iota(jnp.int32, (8, width), 0)
    for k in range(size):
        top, at = k // 8, k % 8
        for part in parts:
            row = part[top][at : at + 1, :]
            scaled = row * (1.0 / row[:, k : k + 1])
            for t in range(top, tall):
                col = part[t][:, k : k + 1]
                if t == top:
                    if at == 7:
                        continue
                    part[t] = part[t] - jnp.where(sub > at, col * scaled, 0.0)
                else:
                    part[t] = part[t] - col * scaled
    out = []
    for part in parts:
        full = jnp.concatenate(part, axis=0)
        left, right = full[:, :size], full[:, size:]
        pivot = jnp.sum(left * eye, axis=1, keepdims=True)
        out.append(right * lax.rsqrt(pivot))
    return out


def inverse_factors(grams):
    size = grams[0].shape[0]
    if size <= BASE:
        return base_inverse(grams)
    half = size // 2
    first = inverse_factors([g[:half, :half] for g in grams])
    lower = [mm(g[half:, :half], w, ((1,), (1,))) for g, w in zip(grams, first)]
    rest = [g[half:, half:] - mm(l, l, ((1,), (1,))) for g, l in zip(grams, lower)]
    second = inverse_factors(rest)
    out = []
    for w1, l21, w2 in zip(first, lower, second):
        below = -mm(w2, mm(l21, w1))
        out.append(
            jnp.concatenate(
                [
                    jnp.concatenate([w1, jnp.zeros_like(w1)], axis=1),
                    jnp.concatenate([below, w2], axis=1),
                ],
                axis=0,
            )
        )
    return out


def factor_kernel(order, total_ref, core_ref, middle_ref):
    w_r, w_c = inverse_factors([total_ref[0], total_ref[1]])
    core = mm(mm(w_r, total_ref[2]), w_c, ((1,), (1,)))
    core_ref[...] = core / jnp.sqrt(F32(order))
    middle_ref[...] = mm(mm(w_r, core, ((0,), (0,))), w_c)


def factor(total, order):
    size = total.shape[-1]
    shape = jax.ShapeDtypeStruct((size, size), F32)
    return pl.pallas_call(
        functools.partial(factor_kernel, order),
        out_shape=(shape, shape),
        in_specs=[pl.BlockSpec(memory_space=pltpu.VMEM)],
        out_specs=(pl.BlockSpec(memory_space=pltpu.VMEM),) * 2,
    )(total)


def split(x):
    high = x.astype(BF16)
    return high, (x - high.astype(F32)).astype(BF16)


def dot(a, b, dims=((1,), (0,))):
    return lax.dot_general(a, b, (dims, ((), ())), preferred_element_type=F32)


def body(order, front, right, left):
    y_part = lax.psum_scatter(dot(front, right), "col", tiled=True).astype(BF16)
    z_part = lax.psum_scatter(dot(front, left, ((0,), (0,))), "row", tiled=True).astype(BF16)
    y = lax.all_gather(y_part, "col", tiled=True)
    z = lax.all_gather(z_part, "row", tiled=True)
    high, low = split(dot(front, z))
    partial = jnp.stack(
        [
            dot(y_part, y_part, ((0,), (0,))),
            dot(z_part, z_part, ((0,), (0,))),
            dot(y, high, ((0,), (0,))) + dot(y, low, ((0,), (0,))),
        ]
    )
    total = lax.psum(partial, ("row", "col"))
    core_scaled, middle = factor(total, order)
    high, low = split(middle)
    projected = (dot(y, high) + dot(y, low)).astype(BF16)
    update = dot(projected, z, ((1,), (1,)))
    residual = (front.astype(F32) - update).astype(BF16)
    return residual, core_scaled


def solution(mesh):
    in_specs = (P("row", "col"), P("col", None), P("row", None))
    out_specs = (P("row", "col"), P())

    def run(front, right, left):
        inner = functools.partial(body, front.shape[0])
        return jax.shard_map(inner, mesh=mesh, in_specs=in_specs, out_specs=out_specs, check_vma=False)(
            front, right, left
        )

    return run
```

```python
import functools

import jax
import jax.numpy as jnp
from jax import lax
from jax.experimental import pallas as pl
from jax.experimental.pallas import tpu as pltpu
from jax.sharding import PartitionSpec as P

F32 = jnp.float32
BF16 = jnp.bfloat16
BASE = 64


def mm(a, b, dims=((1,), (0,))):
    return lax.dot_general(
        a, b, (dims, ((), ())), precision=lax.Precision.HIGHEST, preferred_element_type=F32
    )


def base_inverse(grams):
    size = grams[0].shape[0]
    tall = size // 8
    width = 2 * size
    eye = (
        lax.broadcasted_iota(jnp.int32, (size, size), 0) == lax.broadcasted_iota(jnp.int32, (size, size), 1)
    ).astype(F32)
    wide = [jnp.concatenate([g, eye], axis=1) for g in grams]
    parts = [[w[8 * t : 8 * t + 8] for t in range(tall)] for w in wide]
    sub = lax.broadcasted_iota(jnp.int32, (8, width), 0)
    for k in range(size):
        top, at = k // 8, k % 8
        for part in parts:
            row = part[top][at : at + 1, :]
            scaled = row * (1.0 / row[:, k : k + 1])
            for t in range(top, tall):
                col = part[t][:, k : k + 1]
                if t == top:
                    if at == 7:
                        continue
                    part[t] = part[t] - jnp.where(sub > at, col * scaled, 0.0)
                else:
                    part[t] = part[t] - col * scaled
    out = []
    for part in parts:
        full = jnp.concatenate(part, axis=0)
        left, right = full[:, :size], full[:, size:]
        pivot = jnp.sum(left * eye, axis=1, keepdims=True)
        out.append(right * lax.rsqrt(pivot))
    return out


def inverse_factors(grams):
    size = grams[0].shape[0]
    if size <= BASE:
        return base_inverse(grams)
    half = size // 2
    first = inverse_factors([g[:half, :half] for g in grams])
    lower = [mm(g[half:, :half], w, ((1,), (1,))) for g, w in zip(grams, first)]
    rest = [g[half:, half:] - mm(l, l, ((1,), (1,))) for g, l in zip(grams, lower)]
    second = inverse_factors(rest)
    out = []
    for w1, l21, w2 in zip(first, lower, second):
        below = -mm(w2, mm(l21, w1))
        out.append(
            jnp.concatenate(
                [
                    jnp.concatenate([w1, jnp.zeros_like(w1)], axis=1),
                    jnp.concatenate([below, w2], axis=1),
                ],
                axis=0,
            )
        )
    return out


def factor_kernel(order, total_ref, core_ref, middle_ref):
    size = core_ref.shape[0]
    gram_r, cross, gram_c = (total_ref[:, n].reshape(size, size) for n in range(3))
    w_r, w_c = inverse_factors([gram_r, gram_c])
    core = mm(mm(w_r, cross), w_c, ((1,), (1,)))
    core_ref[...] = core / jnp.sqrt(F32(order))
    middle_ref[...] = mm(mm(w_r, core, ((0,), (0,))), w_c)


def factor(total, order):
    size = total.shape[-1]
    shape = jax.ShapeDtypeStruct((size, size), F32)
    return pl.pallas_call(
        functools.partial(factor_kernel, order),
        out_shape=(shape, shape),
        in_specs=[pl.BlockSpec(memory_space=pltpu.VMEM)],
        out_specs=(pl.BlockSpec(memory_space=pltpu.VMEM),) * 2,
    )(total)


def split(x):
    high = x.astype(BF16)
    return high, (x - high.astype(F32)).astype(BF16)


def dot(a, b, dims=((1,), (0,))):
    return lax.dot_general(a, b, (dims, ((), ())), preferred_element_type=F32)


def greet(groups):
    barrier = pltpu.get_barrier_semaphore()
    for axis, count in groups:
        me = lax.axis_index(axis)
        for step in range(1, count):
            pl.semaphore_signal(
                barrier, inc=1, device_id={axis: lax.rem(me + step, count)}, device_id_type=pl.DeviceIdType.MESH
            )
    pl.semaphore_wait(barrier, sum(count - 1 for _, count in groups))


def scatter(axis, count, source, slots, send, recv):
    me = lax.axis_index(axis)
    copies = []
    for step in range(1, count):
        peer = lax.rem(me + step, count)
        copies.append(
            pltpu.make_async_remote_copy(
                src_ref=source(peer),
                dst_ref=slots.at[step - 1],
                send_sem=send.at[step - 1],
                recv_sem=recv.at[step - 1],
                device_id={axis: peer},
                device_id_type=pl.DeviceIdType.MESH,
            )
        )
    for copy in copies:
        copy.start()
    return copies


def gather(axis, count, blocks, send, recv):
    me = lax.axis_index(axis)
    sends, receives = [], []
    for step in range(1, count):
        for slot, peer, bag in (
            (me, lax.rem(me + step, count), sends),
            (lax.rem(me - step + count, count), lax.rem(me + step, count), receives),
        ):
            bag.append(
                pltpu.make_async_remote_copy(
                    src_ref=blocks.at[me],
                    dst_ref=blocks.at[slot],
                    send_sem=send.at[step - 1],
                    recv_sem=recv.at[step - 1],
                    device_id={axis: peer},
                    device_id_type=pl.DeviceIdType.MESH,
                )
            )
    for copy in sends:
        copy.start()
    return sends, receives


def finish(pair):
    for copy in pair[1]:
        copy.wait_recv()
    for copy in pair[0]:
        copy.wait_send()


def share_kernel(rows, cols, yp_ref, zp_ref, y_ref, z_ref, y_buf, z_buf, *sems):
    greet((("row", rows), ("col", cols)))
    me_r, me_c = lax.axis_index("row"), lax.axis_index("col")
    z_in = scatter("row", rows, lambda k: zp_ref.at[k], z_buf, sems[0], sems[1])
    y_in = scatter("col", cols, lambda k: yp_ref.at[k], y_buf, sems[2], sems[3])
    for copy in z_in:
        copy.wait()
    total = zp_ref[me_r].astype(F32)
    for step in range(rows - 1):
        total = total + z_buf[step].astype(F32)
    z_ref[me_r] = total.astype(BF16)
    z_out = gather("row", rows, z_ref, sems[4], sems[5])
    for copy in y_in:
        copy.wait()
    total = yp_ref[me_c]
    for step in range(cols - 1):
        total = total + y_buf[step]
    y_ref[me_c] = total.astype(BF16)
    y_out = gather("col", cols, y_ref, sems[6], sems[7])
    finish(z_out)
    finish(y_out)


def share(yp, zp):
    cols, y_rows, size = yp.shape
    rows, z_rows, _ = zp.shape
    dma = pltpu.SemaphoreType.DMA
    return pl.pallas_call(
        functools.partial(share_kernel, rows, cols),
        out_shape=(jax.ShapeDtypeStruct(yp.shape, BF16), jax.ShapeDtypeStruct(zp.shape, BF16)),
        in_specs=[pl.BlockSpec(memory_space=pltpu.VMEM)] * 2,
        out_specs=(pl.BlockSpec(memory_space=pltpu.VMEM),) * 2,
        scratch_shapes=[
            pltpu.VMEM((cols - 1, y_rows, size), F32),
            pltpu.VMEM((rows - 1, z_rows, size), BF16),
        ]
        + [dma((n - 1,)) for n in (rows, rows, cols, cols, rows, rows, cols, cols)],
        compiler_params=pltpu.CompilerParams(collective_id=0, has_side_effects=True),
    )(yp, zp)


def total_kernel(rows, cols, both_ref, gram_ref, total_ref, row_buf, own, col_buf, *sems):
    greet((("row", rows), ("col", cols)))
    me_r, me_c = lax.axis_index("row"), lax.axis_index("col")
    height = gram_ref.shape[0]

    def piece(k):
        return both_ref.at[:, pl.ds(pl.multiple_of(k * height, 8), height), :]

    for copy in scatter("row", rows, piece, row_buf, sems[0], sems[1]):
        copy.wait()
    summed = piece(me_r)[...]
    for step in range(rows - 1):
        summed = summed + row_buf[step]
    total_ref[me_r, 0] = summed[0]
    own[0] = summed[1]
    own[1] = gram_ref[...]
    col_buf[cols - 1] = own[...]
    for copy in scatter("col", cols, lambda k: own, col_buf, sems[2], sems[3]):
        copy.wait()
    summed = None
    for member in range(cols):
        slot = lax.rem(me_c - member + 2 * cols - 1, cols)
        summed = col_buf[slot] if summed is None else summed + col_buf[slot]
    total_ref[me_r, 1] = summed[0]
    total_ref[me_r, 2] = summed[1]
    finish(gather("row", rows, total_ref, sems[4], sems[5]))


def total_of(both, gram, rows, cols):
    height, size = gram.shape
    dma = pltpu.SemaphoreType.DMA
    return pl.pallas_call(
        functools.partial(total_kernel, rows, cols),
        out_shape=jax.ShapeDtypeStruct((rows, 3, height, size), F32),
        in_specs=[pl.BlockSpec(memory_space=pltpu.VMEM)] * 2,
        out_specs=pl.BlockSpec(memory_space=pltpu.VMEM),
        scratch_shapes=[
            pltpu.VMEM((rows - 1, 2, height, size), F32),
            pltpu.VMEM((2, height, size), F32),
            pltpu.VMEM((cols, 2, height, size), F32),
        ]
        + [dma((n - 1,)) for n in (rows, rows, cols, cols, rows, rows)],
        compiler_params=pltpu.CompilerParams(collective_id=1, has_side_effects=True),
    )(both, gram)


def body(order, rows, cols, front, right, left):
    size = right.shape[1]
    yp = dot(front, right).reshape(cols, -1, size)
    zp = dot(front, left, ((0,), (0,))).astype(BF16).reshape(rows, -1, size)
    y, z = share(yp, zp)
    y, z = y.reshape(-1, size), z.reshape(-1, size)
    high, low = split(dot(front, z))
    both = jnp.stack([dot(y, y, ((0,), (0,))), dot(y, high, ((0,), (0,))) + dot(y, low, ((0,), (0,)))])
    height = size // rows
    gram = lax.dynamic_slice_in_dim(dot(z, z, ((0,), (0,))), lax.axis_index("row") * height, height)
    core_scaled, middle = factor(total_of(both, gram, rows, cols), order)
    high, low = split(middle)
    projected = (dot(y, high) + dot(y, low)).astype(BF16)
    update = dot(projected, z, ((1,), (1,)))
    residual = (front.astype(F32) - update).astype(BF16)
    return residual, core_scaled


def solution(mesh):
    in_specs = (P("row", "col"), P("col", None), P("row", None))
    out_specs = (P("row", "col"), P())

    def run(front, right, left):
        inner = functools.partial(body, front.shape[0], mesh.shape["row"], mesh.shape["col"])
        return jax.shard_map(inner, mesh=mesh, in_specs=in_specs, out_specs=out_specs, check_vma=False)(
            front, right, left
        )

    return run
```

```python
import functools
import math

import jax
import jax.numpy as jnp
from jax import lax
from jax.experimental import pallas as pl
from jax.experimental.pallas import tpu as pltpu
from jax.sharding import PartitionSpec as P

F32 = jnp.float32
BF16 = jnp.bfloat16
BASE = 64


def mm(a, b, dims=((1,), (0,))):
    return lax.dot_general(
        a, b, (dims, ((), ())), precision=lax.Precision.HIGHEST, preferred_element_type=F32
    )


def base_inverse(grams):
    size = grams[0].shape[0]
    tall = size // 8
    width = 2 * size
    eye = (
        lax.broadcasted_iota(jnp.int32, (size, size), 0) == lax.broadcasted_iota(jnp.int32, (size, size), 1)
    ).astype(F32)
    wide = [jnp.concatenate([g, eye], axis=1) for g in grams]
    parts = [[w[8 * t : 8 * t + 8] for t in range(tall)] for w in wide]
    sub = lax.broadcasted_iota(jnp.int32, (8, width), 0)
    for k in range(size):
        top, at = k // 8, k % 8
        for part in parts:
            row = part[top][at : at + 1, :]
            scaled = row * (1.0 / row[:, k : k + 1])
            for t in range(top, tall):
                col = part[t][:, k : k + 1]
                if t == top:
                    if at == 7:
                        continue
                    part[t] = part[t] - jnp.where(sub > at, col * scaled, 0.0)
                else:
                    part[t] = part[t] - col * scaled
    out = []
    for part in parts:
        full = jnp.concatenate(part, axis=0)
        left, right = full[:, :size], full[:, size:]
        pivot = jnp.sum(left * eye, axis=1, keepdims=True)
        out.append(right * lax.rsqrt(pivot))
    return out


def inverse_factors(grams):
    size = grams[0].shape[0]
    if size <= BASE:
        return base_inverse(grams)
    half = size // 2
    first = inverse_factors([g[:half, :half] for g in grams])
    lower = [mm(g[half:, :half], w, ((1,), (1,))) for g, w in zip(grams, first)]
    rest = [g[half:, half:] - mm(l, l, ((1,), (1,))) for g, l in zip(grams, lower)]
    second = inverse_factors(rest)
    out = []
    for w1, l21, w2 in zip(first, lower, second):
        below = -mm(w2, mm(l21, w1))
        out.append(
            jnp.concatenate(
                [
                    jnp.concatenate([w1, jnp.zeros_like(w1)], axis=1),
                    jnp.concatenate([below, w2], axis=1),
                ],
                axis=0,
            )
        )
    return out


def factor_kernel(order, total_ref, core_ref, middle_ref):
    size = core_ref.shape[0]
    gram_r, cross, gram_c = (total_ref[:, n].reshape(size, size) for n in range(3))
    w_r, w_c = inverse_factors([gram_r, gram_c])
    core = mm(mm(w_r, cross), w_c, ((1,), (1,)))
    core_ref[...] = core / jnp.sqrt(F32(order))
    middle_ref[...] = mm(mm(w_r, core, ((0,), (0,))), w_c)


def factor(total, order):
    size = total.shape[-1]
    shape = jax.ShapeDtypeStruct((size, size), F32)
    return pl.pallas_call(
        functools.partial(factor_kernel, order),
        out_shape=(shape, shape),
        in_specs=[pl.BlockSpec(memory_space=pltpu.VMEM)],
        out_specs=(pl.BlockSpec(memory_space=pltpu.VMEM),) * 2,
    )(total)


def split(x):
    high = x.astype(BF16)
    return high, (x - high.astype(F32)).astype(BF16)


def dot(a, b, dims=((1,), (0,))):
    return lax.dot_general(a, b, (dims, ((), ())), preferred_element_type=F32)


def greet(groups):
    barrier = pltpu.get_barrier_semaphore()
    for axis, count in groups:
        me = lax.axis_index(axis)
        for step in range(1, count):
            pl.semaphore_signal(
                barrier, inc=1, device_id={axis: lax.rem(me + step, count)}, device_id_type=pl.DeviceIdType.MESH
            )
    pl.semaphore_wait(barrier, sum(count - 1 for _, count in groups))


def scatter(axis, count, source, slots, send, recv):
    me = lax.axis_index(axis)
    copies = []
    for step in range(1, count):
        peer = lax.rem(me + step, count)
        copies.append(
            pltpu.make_async_remote_copy(
                src_ref=source(peer),
                dst_ref=slots.at[step - 1],
                send_sem=send.at[step - 1],
                recv_sem=recv.at[step - 1],
                device_id={axis: peer},
                device_id_type=pl.DeviceIdType.MESH,
            )
        )
    for copy in copies:
        copy.start()
    return copies


def gather(axis, count, blocks, send, recv):
    me = lax.axis_index(axis)
    sends, receives = [], []
    for step in range(1, count):
        for slot, peer, bag in (
            (me, lax.rem(me + step, count), sends),
            (lax.rem(me - step + count, count), lax.rem(me + step, count), receives),
        ):
            bag.append(
                pltpu.make_async_remote_copy(
                    src_ref=blocks.at[me],
                    dst_ref=blocks.at[slot],
                    send_sem=send.at[step - 1],
                    recv_sem=recv.at[step - 1],
                    device_id={axis: peer},
                    device_id_type=pl.DeviceIdType.MESH,
                )
            )
    for copy in sends:
        copy.start()
    return sends, receives


def finish(pair):
    for copy in pair[1]:
        copy.wait_recv()
    for copy in pair[0]:
        copy.wait_send()


def hop(source, target, send, recv, peer):
    return pltpu.make_async_remote_copy(
        src_ref=source,
        dst_ref=target,
        send_sem=send,
        recv_sem=recv,
        device_id={"col": peer},
        device_id_type=pl.DeviceIdType.MESH,
    )


def chain_step(step, cols, yp_ref, bufs, send, recv):
    me = lax.axis_index("col")
    for way in range(2):
        place = me if way == 0 else cols - 1 - me
        to = me + 1 if way == 0 else me - 1
        far = cols - 1 - (step - place)
        chunk = far if way == 0 else cols - 1 - far
        buf, s_sem, r_sem = bufs[way], send.at[way, step], recv.at[way, step]

        @pl.when(place == 0)
        def _():
            hop(yp_ref.at[chunk], buf.at[step], s_sem, r_sem, to).start()

        if step > 0:

            @pl.when((place >= 1) & (place <= step))
            def _():
                hop(buf.at[step - 1], buf.at[step - 1], send.at[way, step - 1], recv.at[way, step - 1], to).wait_recv()
                buf[step - 1] = buf[step - 1] + yp_ref[chunk]
                hop(buf.at[step - 1], buf.at[step], s_sem, r_sem, to).start()


def chain_end(cols, yp_ref, y_ref, acc, bufs, send, recv):
    me = lax.axis_index("col")
    last = cols - 2
    acc[...] = yp_ref[me]
    for way in range(2):
        place = me if way == 0 else cols - 1 - me
        came = me - 1 if way == 0 else me + 1
        buf = bufs[way]

        @pl.when(place >= 1)
        def _():
            hop(buf.at[last], buf.at[last], send.at[way, last], recv.at[way, last], came).wait_recv()
            acc[...] = acc[...] + buf[last]

    y_ref[me] = acc[...].astype(BF16)
    for way in range(2):
        place = me if way == 0 else cols - 1 - me
        to = me + 1 if way == 0 else me - 1
        for step in range(cols - 1):

            @pl.when(place <= step)
            def _():
                hop(acc, bufs[way].at[step], send.at[way, step], recv.at[way, step], to).wait_send()


def spread(cols, y_ref, send, recv):
    me = lax.axis_index("col")

    def each(step, act):
        for way in range(2):
            place = me if way == 0 else cols - 1 - me
            sign = 1 if way == 0 else -1
            s_sem, r_sem = send.at[way, step], recv.at[way, step]
            if act == "got":

                @pl.when(place >= step + 1)
                def _():
                    block = y_ref.at[me - sign * (step + 1)]
                    hop(block, block, s_sem, r_sem, me - sign).wait_recv()

            else:

                @pl.when((place >= step) & (place < cols - 1))
                def _():
                    block = y_ref.at[me - sign * step]
                    copy = hop(block, block, s_sem, r_sem, me + sign)
                    if act == "send":
                        copy.start()
                    else:
                        copy.wait_send()

    for step in range(cols - 1):
        each(step, "send")
        each(step, "got")
    for step in range(cols - 1):
        each(step, "sent")


def share_kernel(
    rows, cols, tile, yp_ref, left_ref, front_ref, y_ref, z_ref, zp, z_buf, right_buf, left_buf, acc, tiles, t_sem, *sems
):
    greet((("row", rows), ("col", cols)))
    me_r = lax.axis_index("row")
    chain = (cols, yp_ref, (right_buf, left_buf), sems[2], sems[3])
    z_rows, size = zp.shape[1:]
    count = front_ref.shape[1] // tile
    group = tile // z_rows

    def fetch(t):
        slot = lax.rem(t, 2)
        return pltpu.make_async_copy(
            front_ref.at[:, pl.ds(pl.multiple_of(t * tile, 128), tile)], tiles.at[slot], t_sem.at[slot]
        )

    chain_step(0, *chain)
    fetch(0).start()

    @pl.loop(0, count)
    def _(t):
        @pl.when(t + 1 < count)
        def _():
            fetch(t + 1).start()

        fetch(t).wait()
        part = dot(left_ref[...], tiles[lax.rem(t, 2)]).T.astype(BF16)
        for n in range(group):
            zp[t * group + n] = part[n * z_rows : (n + 1) * z_rows]

    z_in = scatter("row", rows, lambda k: zp.at[k], z_buf, sems[0], sems[1])
    for step in range(1, cols - 1):
        chain_step(step, *chain)
    for copy in z_in:
        copy.wait()
    total = zp[me_r].astype(F32)
    for step in range(rows - 1):
        total = total + z_buf[step].astype(F32)
    z_ref[me_r] = total.astype(BF16)
    z_out = gather("row", rows, z_ref, sems[4], sems[5])
    chain_end(cols, yp_ref, y_ref, acc, (right_buf, left_buf), sems[2], sems[3])
    spread(cols, y_ref, sems[6], sems[7])
    finish(z_out)


def share(yp, left, front, rows):
    cols, y_rows, size = yp.shape
    depth, width = front.shape
    z_rows = width // rows
    tile = z_rows * 128 // math.gcd(z_rows, 128)
    dma = pltpu.SemaphoreType.DMA
    vmem = pl.BlockSpec(memory_space=pltpu.VMEM)
    return pl.pallas_call(
        functools.partial(share_kernel, rows, cols, tile),
        out_shape=(jax.ShapeDtypeStruct(yp.shape, BF16), jax.ShapeDtypeStruct((rows, z_rows, size), BF16)),
        in_specs=[vmem, vmem, pl.BlockSpec(memory_space=pl.ANY)],
        out_specs=(vmem, vmem),
        scratch_shapes=[
            pltpu.VMEM((rows, z_rows, size), BF16),
            pltpu.VMEM((rows - 1, z_rows, size), BF16),
            pltpu.VMEM((cols - 1, y_rows, size), F32),
            pltpu.VMEM((cols - 1, y_rows, size), F32),
            pltpu.VMEM((y_rows, size), F32),
            pltpu.VMEM((2, depth, tile), BF16),
            dma((2,)),
            dma((rows - 1,)),
            dma((rows - 1,)),
            dma((2, cols - 1)),
            dma((2, cols - 1)),
            dma((rows - 1,)),
            dma((rows - 1,)),
            dma((2, cols - 1)),
            dma((2, cols - 1)),
        ],
        compiler_params=pltpu.CompilerParams(collective_id=0, has_side_effects=True),
    )(yp, left, front)


def total_kernel(rows, cols, both_ref, gram_ref, total_ref, row_buf, own, col_buf, *sems):
    greet((("row", rows), ("col", cols)))
    me_r, me_c = lax.axis_index("row"), lax.axis_index("col")
    height = gram_ref.shape[0]

    def piece(k):
        return both_ref.at[:, pl.ds(pl.multiple_of(k * height, 8), height), :]

    for copy in scatter("row", rows, piece, row_buf, sems[0], sems[1]):
        copy.wait()
    summed = piece(me_r)[...]
    for step in range(rows - 1):
        summed = summed + row_buf[step]
    total_ref[me_r, 0] = summed[0]
    own[0] = summed[1]
    own[1] = gram_ref[...]
    col_buf[cols - 1] = own[...]
    for copy in scatter("col", cols, lambda k: own, col_buf, sems[2], sems[3]):
        copy.wait()
    summed = None
    for member in range(cols):
        slot = lax.rem(me_c - member + 2 * cols - 1, cols)
        summed = col_buf[slot] if summed is None else summed + col_buf[slot]
    total_ref[me_r, 1] = summed[0]
    total_ref[me_r, 2] = summed[1]
    finish(gather("row", rows, total_ref, sems[4], sems[5]))


def total_of(both, gram, rows, cols):
    height, size = gram.shape
    dma = pltpu.SemaphoreType.DMA
    return pl.pallas_call(
        functools.partial(total_kernel, rows, cols),
        out_shape=jax.ShapeDtypeStruct((rows, 3, height, size), F32),
        in_specs=[pl.BlockSpec(memory_space=pltpu.VMEM)] * 2,
        out_specs=pl.BlockSpec(memory_space=pltpu.VMEM),
        scratch_shapes=[
            pltpu.VMEM((rows - 1, 2, height, size), F32),
            pltpu.VMEM((2, height, size), F32),
            pltpu.VMEM((cols, 2, height, size), F32),
        ]
        + [dma((n - 1,)) for n in (rows, rows, cols, cols, rows, rows)],
        compiler_params=pltpu.CompilerParams(collective_id=1, has_side_effects=True),
    )(both, gram)


def body(order, rows, cols, front, right, left):
    size = right.shape[1]
    yp = dot(front, right).reshape(cols, -1, size)
    y, z = share(yp, left.T, front, rows)
    y, z = y.reshape(-1, size), z.reshape(-1, size)
    high, low = split(dot(front, z))
    both = jnp.stack([dot(y, y, ((0,), (0,))), dot(y, high, ((0,), (0,))) + dot(y, low, ((0,), (0,)))])
    height = size // rows
    gram = lax.dynamic_slice_in_dim(dot(z, z, ((0,), (0,))), lax.axis_index("row") * height, height)
    core_scaled, middle = factor(total_of(both, gram, rows, cols), order)
    high, low = split(middle)
    projected = (dot(y, high) + dot(y, low)).astype(BF16)
    update = dot(projected, z, ((1,), (1,)))
    residual = (front.astype(F32) - update).astype(BF16)
    return residual, core_scaled


def solution(mesh):
    in_specs = (P("row", "col"), P("col", None), P("row", None))
    out_specs = (P("row", "col"), P())

    def run(front, right, left):
        inner = functools.partial(body, front.shape[0], mesh.shape["row"], mesh.shape["col"])
        return jax.shard_map(inner, mesh=mesh, in_specs=in_specs, out_specs=out_specs, check_vma=False)(
            front, right, left
        )

    return run
```
